512 devices in a mesh: blk: 512 (over x, z, y, core).
Axes of the slice: x: 4, y: 4, z: 16, core: 2. Of those that a mesh axis runs over, the one named last changes fastest.
Arguments:
- rhs: float32 [524288, 256], P('blk'), may hold values from -6 to 6
- diag_inv: float32 [524288, 128], P('blk')
- factor_blocks: float32 [15360, 128, 128], P('blk'), may hold values from -0.125 to 0.125
- order: int32 [4096], P('blk'), may hold values from 0 to 7, as said below
- blk_row: int32 [15360], P('blk'), may hold values from 0 to 4095, as said below
- blk_col: int32 [15360], P('blk'), may hold values from 0 to 4095, as said below
Outputs:
- solution: float32 [524288, 256], P('blk')
The draws below stay inside these ranges and needn't reach their ends.
Inputs may be any that keep to these rules, and one draw needn't show every extreme that they name: `order`: for each device d, entries d * 8 to d * 8 + 7 are a permutation of 0 to 7. `blk_row`: stored block j lies on device j // 30; with p = j % 30 and k = p // 10, its row is a block row of that same device whose level is above k. `blk_col`: with j, p and k as for blk_row and e = (p // 2) % 5, the 2 blocks that share j // 30, k and e have as columns, each once, the 2 block rows of level k of the device e places below j // 30, counted cyclically over all devices.
All inputs are finite; a program needn't handle non-finite values.
Results may differ from the reference program's by a relative error of at most 0.0001.
Values sent between devices are 32-bit elements; how exact they have to be, the bound alone decides.
No kernel may reach another device: no remote copies, remote signals or barrier semaphores. Data moves between devices by JAX's collectives and lax.ppermute only.
A program may use at most 64 MiB of HBM per device.

```python
import math
import jax
import jax.numpy as jnp
from jax import lax

BS = 128
RHS = 256
LANES = 2
STEPS = 4
BAND = 4
R = 8
NOFF = 30
NB = 4096
NROWS = 524288
N_BLK = 512


def pattern(key):
    perm_keys = jax.random.split(jax.random.fold_in(key, 11), N_BLK)
    orders = jax.vmap(lambda single: jax.random.permutation(single, R))(perm_keys).astype(jnp.int32)
    indices = jnp.arange(NOFF, dtype=jnp.int32)
    step_of = indices // ((BAND + 1) * LANES)
    offset_of = indices // LANES % (BAND + 1)
    lane_of = indices % LANES
    devices = jnp.arange(N_BLK, dtype=jnp.int32)[:, None]
    owners = (devices - offset_of[None, :]) % N_BLK
    col_slot = orders[owners, (step_of * LANES + lane_of)[None, :]]
    columns = owners * R + col_slot
    spread = (STEPS - 1 - step_of)[None, :]
    row_level = jax.random.randint(jax.random.fold_in(key, 12), (N_BLK, NOFF), 0, 1 << 20) % spread + step_of[None, :] + 1
    row_lane = jax.random.randint(jax.random.fold_in(key, 13), (N_BLK, NOFF), 0, LANES)
    row_slot = jnp.take_along_axis(orders, row_level * LANES + row_lane, axis=1)
    rows_out = devices * R + row_slot
    return (orders.reshape(-1), rows_out.reshape(-1).astype(jnp.int32), columns.reshape(-1).astype(jnp.int32))


def draw_order(key, part):
    return pattern(key)[0]


def draw_blk_row(key, part):
    return pattern(key)[1]


def draw_blk_col(key, part):
    return pattern(key)[2]


def draw_diag_inv(key, part):
    row_index = jnp.arange(NB * BS, dtype=jnp.int32) % BS
    identity = (row_index[:, None] == jnp.arange(BS, dtype=jnp.int32)[None, :]).astype(jnp.float32)
    noise_part = jax.random.normal(key, (NB * BS, BS), jnp.float32) * (0.5 / math.sqrt(BS))
    return identity + noise_part


def steps_of(rng, shape, cuts, least, top_value):
    loudness, own = 1.0, jax.random.fold_in(rng, 6)
    for axis_at, blocks in cuts:
        draws = jnp.exp(jax.random.uniform(jax.random.fold_in(own, axis_at), (blocks,), jnp.float32, least / len(cuts), top_value / len(cuts)))
        loudness = loudness * jnp.repeat(draws, shape[axis_at] // blocks).reshape([-1 if axis == axis_at else 1 for axis in range(len(shape))])
    return loudness


def scatter_about(key, dims, scale, reach, cuts=(), kind=jnp.bfloat16):
    gain = steps_of(key, dims, cuts, -0.22, 0.18) if cuts else 1.0
    array = jax.random.normal(key, dims, jnp.float32) * scale * gain
    return jnp.minimum(jnp.maximum(array, -reach), reach).astype(kind)


def setup_inputs(seed: int = 0) -> dict:
    streams_of = jax.random.split(jax.random.key(seed), 7)
    return {
        "rhs": scatter_about(streams_of[0], (NROWS, RHS), 1.0, 6.0, ((0, 512),), jnp.float32),
        "diag_inv": draw_diag_inv(jax.random.fold_in(streams_of[6], 71), 0),
        "factor_blocks": scatter_about(streams_of[2], (NOFF * N_BLK, BS, BS), (16 * BS) ** -0.5, 0.125, ((0, 512),), jnp.float32),
        "order": draw_order(jax.random.fold_in(streams_of[6], 71), 0),
        "blk_row": draw_blk_row(jax.random.fold_in(streams_of[6], 71), 0),
        "blk_col": draw_blk_col(jax.random.fold_in(streams_of[6], 71), 0),
    }


def reference(rhs, diag_inv, factor_blocks, order, blk_row, blk_col):
    block_rows = rhs.reshape(NB, BS, RHS)
    inverses = diag_inv.reshape(NB, BS, BS)
    positions = jnp.arange(NB, dtype=jnp.int32)
    owners = positions // R
    level_at = ((positions % R) // LANES).astype(jnp.int32)
    levels = jnp.zeros((NB,), jnp.int32).at[owners * R + order.astype(jnp.int32)].set(level_at)
    residual = block_rows.astype(jnp.float32)
    solution = jnp.zeros((NB, BS, RHS), jnp.float32)
    column_levels = levels[blk_col]
    for step_index in range(STEPS):
        rows_now = jnp.nonzero(levels == step_index, size=N_BLK * LANES)[0].astype(jnp.int32)
        solved = jnp.einsum("nij,njc->nic", inverses[rows_now], residual[rows_now], precision=lax.Precision.HIGHEST)
        solution = solution.at[rows_now].set(solved)
        if step_index + 1 < STEPS:
            chosen = jnp.nonzero(column_levels == step_index, size=N_BLK * (BAND + 1) * LANES)[0].astype(jnp.int32)
            chosen = chosen.reshape(BAND + 1, N_BLK * LANES)

            def apply_group(carried, picked):
                contribution = jnp.einsum("nij,njc->nic", factor_blocks[picked], solution[blk_col[picked]], precision=lax.Precision.HIGHEST)
                return carried.at[blk_row[picked]].add(-contribution), None

            residual, _ = lax.scan(apply_group, residual, chosen)
    return solution.reshape(NROWS, RHS)
```

```python
import jax
import jax.numpy as jnp
from jax import lax
from jax.experimental import pallas as pl
from jax.experimental.pallas import tpu as pltpu
from jax.sharding import PartitionSpec as P

BS = 128
RHS = 256
LANES = 2
STEPS = 4
BAND = 4
R = 8
GROUP = (BAND + 1) * LANES

VMEM = pl.BlockSpec(memory_space=pltpu.VMEM)
SMEM = pl.BlockSpec(memory_space=pltpu.SMEM)
ANY = pl.BlockSpec(memory_space=pl.ANY)
HBM = pl.BlockSpec(memory_space=pltpu.HBM)


def halves(value):
    high = value.astype(jnp.bfloat16)
    low = (value - high.astype(jnp.float32)).astype(jnp.bfloat16)
    return high, low


def left(value):
    high, low = halves(value)
    return jnp.concatenate([high, high, low], axis=1)


def right(value):
    high, low = halves(value)
    return jnp.concatenate([high, low, high], axis=0)


def dot(a, b):
    return jnp.dot(a, b, preferred_element_type=jnp.float32)


def slot_at(order, p):
    a, b = order[p - p % 2], order[p - p % 2 + 1]
    return jnp.maximum(a, b) if p % 2 else jnp.minimum(a, b)


def block_of(blk_col, step, offset, lane):
    first = step * GROUP + offset * LANES
    swapped = (blk_col[first] > blk_col[first + 1]).astype(jnp.int32)
    return first + (swapped if lane == 0 else 1 - swapped)


def weights(order, blk_row, blk_col, f_ref, blocks, positions):
    slots = [slot_at(order, p) for p in positions]
    columns = []
    for step, offset, lane in blocks:
        j = block_of(blk_col, step, offset, lane)
        own = left(f_ref[j])
        row = lax.rem(blk_row[j], R)
        columns.append(
            jnp.concatenate(
                [jnp.where(row == s, own, jnp.zeros_like(own)) for s in slots], axis=0
            )
        )
    return columns


def spread(order, blk_row, blk_col, f_ref, terms, positions):
    columns = weights(order, blk_row, blk_col, f_ref, [t[:3] for t in terms], positions)
    return dot(
        jnp.concatenate(columns, axis=1),
        jnp.concatenate([right(t[3]) for t in terms], axis=0),
    )


def copies(pairs, sems):
    made = [pltpu.make_async_copy(s, d, sems.at[i]) for i, (s, d) in enumerate(pairs)]
    for c in made:
        c.start()
    return made


def first_kernel(order, rhs, diag, x_ref, res, inv, sems):
    pairs = []
    for lane in range(LANES):
        slot = slot_at(order, lane)
        pairs += [(rhs.at[slot], res.at[lane]), (diag.at[slot], inv.at[lane])]
    made = copies(pairs, sems)
    for c in made:
        c.wait()
    for lane in range(LANES):
        x_ref[lane] = dot(left(inv[lane]), right(res[lane]))


def solve_kernel(step, order, blk_row, blk_col, f_ref, diag, res, far2, far4, near, *rest):
    if step == STEPS - 1:
        _, out, x_ref, inv, sems, out_sems = rest
    else:
        x_ref, inv, sems = rest
    slots = [slot_at(order, step * LANES + lane) for lane in range(LANES)]
    made = copies([(diag.at[slots[l]], inv.at[l]) for l in range(LANES)], sems)
    sources = {1: near.at[0], 2: far2, 3: near.at[1], 4: far4}
    terms = [
        (step - 1, e, lane, sources[e][lane])
        for e in range(1, BAND + 1)
        for lane in range(LANES)
    ]
    positions = range(step * LANES, (step + 1) * LANES)
    total = spread(order, blk_row, blk_col, f_ref, terms, positions)
    base = res.shape[0] - (R - step * LANES)
    for c in made:
        c.wait()
    for lane in range(LANES):
        rest_of = res[base + lane] - total[lane * BS : (lane + 1) * BS]
        x_ref[lane] = dot(left(inv[lane]), right(rest_of))
    if step == STEPS - 1:
        made = copies([(x_ref.at[l], out.at[slots[l]]) for l in range(LANES)], out_sems)
        for c in made:
            c.wait()


def window_kernel(step, order, blk_row, blk_col, f_ref, x_ref, *rest):
    slots = [slot_at(order, step * LANES + lane) for lane in range(LANES)]
    if step == 0:
        rhs, out, new, res, sems, out_sems = rest
        made = copies(
            [(rhs.at[slot_at(order, p)], res.at[p - LANES]) for p in range(LANES, R)], sems
        )
        base = 0
        terms = []
    else:
        res, far2, far4, near, _, out, new, out_sems = rest
        made = []
        base = LANES
        sources = {1: near.at[0], 2: far2, 3: near.at[1], 4: far4}
        terms = [
            (step - 1, e, lane, sources[e][lane])
            for e in range(1, BAND + 1)
            for lane in range(LANES)
        ]
    out_made = copies([(x_ref.at[l], out.at[slots[l]]) for l in range(LANES)], out_sems)
    terms += [(step, 0, lane, x_ref[lane]) for lane in range(LANES)]
    positions = range((step + 1) * LANES, R)
    total = spread(order, blk_row, blk_col, f_ref, terms, positions)
    for c in made:
        c.wait()
    for i in range(len(positions)):
        new[i] = res[base + i] - total[i * BS : (i + 1) * BS]
    for c in out_made:
        c.wait()


def body(rhs, diag_inv, factor_blocks, order, blk_row, blk_col):
    f32 = jnp.float32
    rhs = rhs.reshape(R, BS, RHS)
    diag = diag_inv.reshape(R, BS, BS)
    count = lax.axis_size("blk")
    odd = lax.rem(lax.axis_index("blk"), 2) == 1
    pair = jax.ShapeDtypeStruct((LANES, BS, RHS), f32)
    whole = jax.ShapeDtypeStruct((R, BS, RHS), f32)
    dma = pltpu.SemaphoreType.DMA
    params = pltpu.CompilerParams(vmem_limit_bytes=24 << 20)

    def shift(value, distance):
        return lax.ppermute(value, "blk", [(i, (i + distance) % count) for i in range(count)])

    def swap(value):
        return lax.ppermute(value, "blk", [(i, i ^ 1) for i in range(count)])

    def cost(blocks, rows):
        return pl.CostEstimate(
            flops=6 * blocks * rows * BS * BS * RHS, bytes_accessed=3 << 20, transcendentals=0
        )

    x = pl.pallas_call(
        first_kernel,
        out_shape=pair,
        in_specs=[SMEM, HBM, HBM],
        out_specs=VMEM,
        scratch_shapes=[
            pltpu.VMEM((LANES, BS, RHS), f32),
            pltpu.VMEM((LANES, BS, BS), f32),
            dma((2 * LANES,)),
        ],
        compiler_params=params,
        name="first",
    )(order, rhs, diag)
    far2 = shift(x, 2)
    far4 = shift(x, 4)
    res, near, out = None, None, None
    last = None
    for step in range(STEPS - 1):
        later = R - (step + 1) * LANES
        new_shape = jax.ShapeDtypeStruct((later, BS, RHS), f32)

        def window(*args, step=step):
            return window_kernel(step, *args)

        if step == 0:
            out, res = pl.pallas_call(
                window,
                out_shape=(whole, new_shape),
                in_specs=[SMEM] * 3 + [VMEM, VMEM, ANY],
                out_specs=(ANY, VMEM),
                scratch_shapes=[
                    pltpu.VMEM((R - LANES, BS, RHS), f32),
                    dma((R - LANES,)),
                    dma((LANES,)),
                ],
                compiler_params=params,
                cost_estimate=cost(2, 6),
                name="window0",
            )(order, blk_row, blk_col, factor_blocks, x, rhs)
        else:
            out, res = pl.pallas_call(
                window,
                out_shape=(whole, new_shape),
                in_specs=[SMEM] * 3 + [VMEM] * 6 + [ANY],
                out_specs=(ANY, VMEM),
                scratch_shapes=[dma((LANES,))],
                input_output_aliases={9: 0},
                compiler_params=params,
                cost_estimate=cost(10, R - (step + 1) * LANES),
                name=f"window{step}",
            )(order, blk_row, blk_col, factor_blocks, x, res, *last, out)
        x, res = lax.optimization_barrier((x, res))
        payload = jnp.where(odd, jnp.stack([far2, far4]), jnp.stack([x, far2]))
        near = swap(payload)
        last = (far2, far4, near)

        def solve(*args, step=step + 1):
            return solve_kernel(step, *args)

        end = step + 1 == STEPS - 1
        scratch = [pltpu.VMEM((LANES, BS, BS), f32), dma((LANES,))]
        if end:
            scratch = [pltpu.VMEM((LANES, BS, RHS), f32)] + scratch + [dma((LANES,))]
        got = pl.pallas_call(
            solve,
            out_shape=whole if end else pair,
            in_specs=[SMEM] * 3 + [VMEM, ANY] + [VMEM] * 4 + ([ANY] if end else []),
            out_specs=ANY if end else VMEM,
            scratch_shapes=scratch,
            input_output_aliases={9: 0} if end else {},
            compiler_params=params,
            name=f"solve{step + 1}",
        )(order, blk_row, blk_col, factor_blocks, diag, res, *last, *([out] if end else []))
        if end:
            return got.reshape(R * BS, RHS)
        x = got
        far2 = shift(x, 2)
        far4 = shift(x, 4)


def solution(mesh):
    placed = (P("blk", None), P("blk", None), P("blk", None, None), P("blk"), P("blk"), P("blk"))
    return jax.shard_map(
        body, mesh=mesh, in_specs=placed, out_specs=P("blk", None), check_vma=False
    )
```
